32 devices in a mesh: group: 2 (over x), tensor: 16 (over z, y, core).
Axes of the slice: x: 2, y: 2, z: 4, core: 2. Of those that a mesh axis runs over, the one named last changes fastest.
Arguments:
- hidden_in: bfloat16 [256, 2048], P(('group', 'tensor')), parts along dimension 0, may hold values from -6 to 6
- queries: bfloat16 [1024, 2048], P(('group', 'tensor')), parts along dimension 0, may hold values from -6 to 6
- kv_cache: bfloat16 [1024, 64, 256], P(('group', 'tensor')), parts along dimension 0, may hold values from -6 to 6
- new_kv: bfloat16 [1024, 256], P(('group', 'tensor')), parts along dimension 0, may hold values from -8 to 8
- cycle_pos: int32 [256], P('group'), parts along dimension 0, may hold values from 0 to 59
- out_weight: bfloat16 [8192, 2048], P('tensor'), may hold values from -0.125 to 0.125
- norm_gain: float32 [2048], replicated, may hold values from 0.1 to 1.9
- route_logits: float32 [256, 8], P(('group', 'tensor')), parts along dimension 0, may hold values from -6 to 303
- expert_ids: int32 [256, 8], P(('group', 'tensor')), parts along dimension 0, may hold values from 0 to 15, all different within a row; in each aligned block of 8 rows (0 to 7, 8 to 15, ...) at most 8 rows name the same one
- expert_in: bfloat16 [16, 2048, 1536], P('tensor'), may hold values from -0.125 to 0.125
- expert_out: bfloat16 [16, 768, 2048], P('tensor'), may hold values from -0.21875 to 0.21875
Outputs:
- hidden_out: bfloat16 [256, 2048], P(('group', 'tensor')), parts along dimension 0
- new_cache: bfloat16 [1024, 64, 256], P(('group', 'tensor')), parts along dimension 0
The draws below stay inside these ranges and needn't reach their ends.
There are 2 independent parts, one for each index of `group`. The reference program is written for one: setup_inputs(seed, part) draws one part's arguments, and reference() takes and returns one part's arrays. A program takes and returns all parts, laid end to end along the dimension named above; an argument that names none is the same for every part. Nothing has to cross between parts.
Inputs may be any that keep to these rules, and one draw needn't show every extreme that they name: `expert_ids`: among the rows of one device no expert is named more than 8 times, a bound that some block reaches there in some device's rows. The 8 experts of a row differ.
All inputs are finite; a program needn't handle non-finite values.
Results may differ from the reference program's by a relative error of at most 0.0063.
Values may be sent and summed in bfloat16 or wider, within the bound.
A program may use at most 64 MiB of HBM per device.

```python
import math
import jax
import jax.numpy as jnp
import numpy as np
from jax import lax

D = 2048
FF = 768
HD = 128
KVH = 4
HQ = 64
TOP = 8
SINK = 4
WIN = 60
STR_DEV = 8
STREAMS = 128
EXPERTS = 16
G = 16
SLOTS = 64
CAP = 8
N_TENSOR = 16


def draw_queries(key, part):
    own_key = jax.random.fold_in(key, 3)
    row_count = KVH * STREAMS
    backdrop = jnp.clip(jax.random.normal(own_key, (row_count, G * HD)), -6.0, 6.0)
    return backdrop.astype(jnp.bfloat16)


def draw_kv_cache(key, part):
    own_key = jax.random.fold_in(key, 5)
    row_count = KVH * STREAMS
    backdrop = jnp.clip(jax.random.normal(own_key, (row_count, SLOTS, 2 * HD)), -6.0, 6.0)
    return backdrop.astype(jnp.bfloat16)


def draw_route_logits(key, part):
    own_key = jax.random.fold_in(key, 7)
    key_base = jax.random.fold_in(own_key, 0)
    return jnp.clip(1.5 * jax.random.normal(key_base, (STREAMS, TOP)), -6.0, 6.0).astype(jnp.float32)


def draw_hidden_in(key, part):
    own_key = jax.random.fold_in(key, 9)
    key_base = jax.random.fold_in(own_key, 0)
    backdrop = jax.random.normal(key_base, (STREAMS, D))
    return jnp.clip(0.7 * backdrop, -6.0, 6.0).astype(jnp.bfloat16)


def place_ends(array, key, least, top_value):
    longest = array.shape.index(max(array.shape))
    spots = []
    for shift in (0, 1):
        where = [jax.random.randint(jax.random.fold_in(key, axis), (), 0, length) for axis, length in enumerate(array.shape)]
        where[longest] = (where[longest] + shift) % array.shape[longest]
        spots.append(tuple(where))
    return array.at[spots[0]].set(least).at[spots[1]].set(top_value)


def levels(stream_key, extent, pieces, least, high):
    def one(axis_at, blocks):
        steps = jax.random.uniform(jax.random.fold_in(jax.random.fold_in(stream_key, 6), axis_at), (blocks,), jnp.float32, least / len(pieces), high / len(pieces))
        return jnp.repeat(jnp.exp(steps), extent[axis_at] // blocks).reshape((-1,) + (1,) * (len(extent) - axis_at - 1))

    gain = one(*pieces[0])
    for cut in pieces[1:]:
        gain = gain * one(*cut)
    return gain


def assign_block(rng, own, number, rows, number_of, top, bound, skew):
    sequence = jax.random.permutation(rng, number_of)
    heavy_load, ordinary = shares(number_of, rows * top, bound, skew, True), shares(number_of, rows * top, bound, skew, False)
    places = jnp.arange(number_of)

    def named(lengths, turn):
        used = int((lengths > 0).sum())
        fixed = max(1, used // 4)
        shifted = fixed + (places - fixed + turn * (used - fixed)) % max(1, number_of - fixed)
        return jnp.zeros((number_of,), jnp.int32).at[sequence[jnp.where(places < fixed, places, shifted)]].set(jnp.asarray(lengths, jnp.int32))

    lengths = jnp.where(number % 4 == 0, named(heavy_load, number // 4), named(ordinary, number - number // 4 - 1))
    mixed = jax.random.permutation(jax.random.fold_in(own, 3), number_of)
    giver, sink = mixed[0:number_of // 2 * 2:2], mixed[1:number_of // 2 * 2:2]
    slack = jnp.minimum(lengths[giver] - 1, bound - lengths[sink]) // 2
    slack = jnp.where((giver == sequence[0]) | (sink == sequence[0]) | (lengths[sink] == 0), 0, jnp.maximum(slack, 0))
    shifted = jax.random.randint(jax.random.fold_in(own, 4), (number_of // 2,), 0, 1 << 20) % (slack + 1)
    lengths = lengths.at[giver].add(-shifted).at[sink].add(shifted)
    items = jnp.searchsorted(jnp.cumsum(lengths), jnp.arange(rows * top), side="right").astype(jnp.int32)
    grid = items.reshape(top, rows).T
    grid = grid[jax.random.permutation(jax.random.fold_in(own, 1), rows)]
    turn = jax.random.randint(jax.random.fold_in(own, 2), (rows, 1), 0, top)
    return jnp.take_along_axis(grid, (jnp.arange(top)[None, :] + turn) % top, axis=1)


def shares(number_of, total, limit, lean, full):
    loads = [(1 << 20) // math.isqrt(standing ** lean) + 1 for standing in range(1, number_of + 1)]
    largest = limit if full else min(limit, max(-(-total // number_of), total * loads[0] // sum(loads)))
    least = 1 if total - largest >= number_of - 1 else 0
    holding, surplus = [largest] + [least] * (number_of - 1), total - largest - least * (number_of - 1)
    while surplus > 0:
        free = [i for i in range(1, number_of) if holding[i] < largest] or [i for i in range(1, number_of) if holding[i] < limit]
        whole, budget = sum([loads[i] for i in free]), surplus
        for i in free:
            addition = min(limit - holding[i], max(1, budget * loads[i] // whole), surplus)
            holding[i] = holding[i] + addition
            surplus = surplus - addition
    return np.array(holding)


def gaussian(key, dims, spread, limit, cuts=(), held_as=jnp.bfloat16):
    drawn = spread * jax.random.normal(key, dims, jnp.float32)
    if cuts:
        drawn = drawn * levels(key, dims, cuts, -0.22, 0.18)
    return jnp.clip(drawn, -limit, limit).astype(held_as)


def setup_inputs(seed: int = 0, part: int = 0) -> dict:
    seeds = jax.random.split(jax.random.key(seed), 12)
    part_keys = jax.random.split(jax.random.fold_in(seeds[11], part), 12)
    hidden_in = draw_hidden_in(jax.random.fold_in(jax.random.fold_in(seeds[11], part), 71), part)
    queries = draw_queries(jax.random.fold_in(jax.random.fold_in(seeds[11], part), 71), part)
    kv_cache = draw_kv_cache(jax.random.fold_in(jax.random.fold_in(seeds[11], part), 71), part)
    new_kv = gaussian(part_keys[3], (KVH * STREAMS, 2 * HD), 2.0, 8.0, ((0, 16),))
    cycle_pos = place_ends(jax.random.randint(part_keys[4], (STREAMS,), 0, WIN), jax.random.fold_in(part_keys[4], 1), 0, WIN - 1).astype(jnp.int32)
    out_weight = gaussian(seeds[5], (HQ * HD, D), (HQ * HD // 4) ** -0.5, 0.125, ((0, 16),))
    norm_gain = jnp.clip(1.0 + 0.18 * jax.random.normal(seeds[6], (D,), jnp.float32), 0.1, 1.9)
    route_logits = draw_route_logits(jax.random.fold_in(jax.random.fold_in(seeds[11], part), 71), part)
    expert_ids_keys = jax.random.split(jax.random.fold_in(part_keys[8], 1), STREAMS // STR_DEV)
    expert_ids_turns = jax.random.permutation(jax.random.fold_in(part_keys[8], 3), STREAMS // STR_DEV)
    expert_ids = jax.vmap(lambda own, number: assign_block(jax.random.fold_in(part_keys[8], 2), own, number, STR_DEV, EXPERTS, TOP, CAP, 3))(expert_ids_keys, expert_ids_turns).reshape((STREAMS, TOP))
    expert_in = gaussian(seeds[9], (EXPERTS, D, 2 * FF), D ** -0.5, 0.125, ((0, 16),))
    expert_out = gaussian(seeds[10], (EXPERTS, FF, D), FF ** -0.5, 0.21875, ((0, 16),))
    return {"hidden_in": hidden_in, "queries": queries, "kv_cache": kv_cache, "new_kv": new_kv, "cycle_pos": cycle_pos, "out_weight": out_weight, "norm_gain": norm_gain, "route_logits": route_logits, "expert_ids": expert_ids, "expert_in": expert_in, "expert_out": expert_out}


def reference(hidden_in, queries, kv_cache, new_kv, cycle_pos, out_weight, norm_gain, route_logits, expert_ids, expert_in, expert_out):
    row_count = KVH * STREAMS
    slot_index = (jnp.repeat(cycle_pos, KVH) + SINK).astype(jnp.int32)
    write_mask = lax.broadcasted_iota(jnp.int32, (row_count, SLOTS), 1) == slot_index[:, None]
    new_cache = jnp.where(write_mask[:, :, None], new_kv[:, None, :], kv_cache)
    key_part = new_cache[:, :, :HD].astype(jnp.float32)
    value_part = new_cache[:, :, HD:].astype(jnp.float32)
    query_heads = queries.reshape(row_count, G, HD).astype(jnp.float32)
    scores = jnp.einsum('rhk,rsk->rhs', query_heads, key_part) / math.sqrt(HD)
    peak = lax.optimization_barrier(jnp.max(scores, axis=-1, keepdims=True))
    weights = jnp.exp(scores - peak)
    attn_probs = (weights / lax.optimization_barrier(jnp.sum(weights, axis=-1, keepdims=True))).astype(jnp.bfloat16)
    head_out = jnp.einsum('rhs,rsk->rhk', attn_probs.astype(jnp.float32), value_part).astype(jnp.bfloat16)
    attention = head_out.reshape(STREAMS, HQ * HD)
    attn_proj = jnp.dot(attention, out_weight, preferred_element_type=jnp.float32)
    mid_state = (hidden_in.astype(jnp.float32) + attn_proj).astype(jnp.bfloat16)
    mid_wide = mid_state.astype(jnp.float32)
    normed = (mid_wide * lax.rsqrt(lax.optimization_barrier(jnp.mean(mid_wide * mid_wide, axis=-1, keepdims=True)) + 1e-06) * norm_gain).astype(jnp.bfloat16)
    gate_probs = jax.nn.softmax(route_logits.astype(jnp.float32), axis=-1).astype(jnp.bfloat16)
    slot_count = N_TENSOR * CAP

    def one_expert(moe_total, expert):
        matches = expert_ids == expert
        chosen = jnp.any(matches, axis=1)
        weight_tok = lax.optimization_barrier(jnp.sum(jnp.where(matches, gate_probs.astype(jnp.float32), jnp.float32(0.0)), axis=1))
        picked_rows = jnp.nonzero(chosen, size=slot_count, fill_value=0)[0].astype(jnp.int32)
        filled = jnp.arange(slot_count, dtype=jnp.int32) < jnp.sum(chosen.astype(jnp.int32))
        rows_in = normed[picked_rows]
        joined = jnp.dot(rows_in, expert_in[expert], preferred_element_type=jnp.float32)
        activated = (jax.nn.silu(joined[:, :FF]) * joined[:, FF:]).astype(jnp.bfloat16)
        result = jnp.dot(activated, expert_out[expert], preferred_element_type=jnp.float32).astype(jnp.bfloat16)
        factor = jnp.where(filled, weight_tok[picked_rows], jnp.float32(0.0))
        moe_total = moe_total.at[picked_rows].add(factor[:, None] * result.astype(jnp.float32))
        return (moe_total, None)
    moe_total, _ = lax.scan(one_expert, jnp.zeros((STREAMS, D), jnp.float32), jnp.arange(EXPERTS, dtype=jnp.int32))
    hidden_out = (mid_state.astype(jnp.float32) + moe_total).astype(jnp.bfloat16)
    return (hidden_out, new_cache)
```

```python
import functools
import math

import jax
import jax.numpy as jnp
from jax import lax
from jax.experimental import pallas as pl
from jax.experimental.pallas import tpu as pltpu
from jax.sharding import PartitionSpec as P

HD = 128
SINK = 4
CHUNKS = 4
MESH = pl.DeviceIdType.MESH


def wait_bytes(ref, sem):
    pltpu.make_async_copy(ref, ref, sem).wait()


def layer_kernel(
    n,
    by_head,
    hidden_in,
    norm_gain,
    route_logits,
    expert_ids,
    out_weight,
    expert_in,
    expert_out,
    hidden_out,
    w_proj,
    w_in,
    w_out,
    heads,
    core_out,
    core_in,
    mine,
    chip_out,
    chip_in,
    gathered,
    act,
    load_sem,
    head_send,
    head_recv,
    core_send,
    core_recv,
    chip_send,
    chip_recv,
    ag_send,
    ag_recv,
    relay_send,
    relay_recv,
):
    me = lax.axis_index("tensor")
    chips = n // 2
    chip, core = me // 2, me % 2
    partner = chip * 2 + (1 - core)
    tokens, width = hidden_in.shape
    part = width // CHUNKS
    ff = w_out.shape[0]
    half = chips * tokens

    barrier = pltpu.get_barrier_semaphore()

    @pl.loop(1, n)
    def _(k):
        pl.semaphore_signal(
            barrier, inc=1, device_id={"tensor": lax.rem(me + k, n)}, device_id_type=MESH
        )

    loads = [
        pltpu.make_async_copy(out_weight, w_proj, load_sem.at[0]),
        pltpu.make_async_copy(expert_in.at[0], w_in, load_sem.at[1]),
        pltpu.make_async_copy(expert_out.at[0], w_out, load_sem.at[2]),
    ]
    for load in loads:
        load.start()
    pl.semaphore_wait(barrier, n - 1)

    def slot(device):
        return lax.rem(device, 2) * chips + device // 2

    my_slot = slot(me)

    @pl.loop(1, n)
    def _(k):
        to = lax.rem(me + k, n)
        pltpu.make_async_remote_copy(
            src_ref=by_head.at[to],
            dst_ref=heads.at[my_slot],
            send_sem=head_send,
            recv_sem=head_recv,
            device_id={"tensor": to},
            device_id_type=MESH,
        ).start()

    heads[my_slot] = by_head[me]

    logits = route_logits[...]
    top = logits.shape[1]
    powers = jnp.exp(logits - jnp.max(logits, axis=-1, keepdims=True))
    gate = (powers / jnp.sum(powers, axis=-1, keepdims=True)).astype(jnp.bfloat16)
    gate = gate.astype(jnp.float32)
    pad = gathered.shape[2] - width
    lanes = lax.broadcasted_iota(jnp.int32, (tokens, pad), 1)
    ids = expert_ids[...]
    table = jnp.zeros((tokens, pad), jnp.float32)
    for j in range(top):
        table = table + jnp.where(lanes == ids[:, j : j + 1], gate[:, j : j + 1], 0.0)
    gathered[my_slot, :, width:] = table.astype(jnp.bfloat16)

    def rows_of(ref, lo, hi):
        other = ref[pl.ds((1 - core) * chips, chips), :, lo:hi].astype(jnp.float32)
        own = ref[pl.ds(core * chips, chips), :, lo:hi].astype(jnp.float32)
        return jnp.concatenate(
            [other.reshape(half, hi - lo), own.reshape(half, hi - lo)], axis=0
        )

    def core_copy(r, k):
        return pltpu.make_async_remote_copy(
            src_ref=core_out.at[r, k],
            dst_ref=core_in.at[r, k],
            send_sem=core_send.at[r, k],
            recv_sem=core_recv.at[r, k],
            device_id={"tensor": partner},
            device_id_type=MESH,
        )

    def reduce_scatter(r, term):
        for k in range(CHUNKS):
            value = term(k)
            core_out[r, k] = value[:half].reshape(chips, tokens, part).astype(jnp.bfloat16)
            core_copy(r, k).start()
            mine[k] = value[half:].reshape(chips, tokens, part)
        for k in range(CHUNKS):
            core_copy(r, k).wait_recv()
            both = (mine[k] + core_in[r, k].astype(jnp.float32)).astype(jnp.bfloat16)
            chip_out[r, k] = both

            @pl.loop(1, chips)
            def _(step):
                to = lax.rem(chip + step, chips)
                pltpu.make_async_remote_copy(
                    src_ref=chip_out.at[r, k, to],
                    dst_ref=chip_in.at[r, k, chip],
                    send_sem=chip_send.at[r],
                    recv_sem=chip_recv.at[r, k],
                    device_id={"tensor": to * 2 + core},
                    device_id_type=MESH,
                ).start()

            chip_in[r, k, chip] = chip_out[r, k, chip]
        sums = []
        for k in range(CHUNKS):
            wait_bytes(chip_in.at[r, k, pl.ds(0, chips - 1)], chip_recv.at[r, k])
            sums.append(jnp.sum(chip_in[r, k].astype(jnp.float32), axis=0))
        return jnp.concatenate(sums, axis=-1)

    wait_bytes(heads.at[pl.ds(0, n - 1)], head_recv)
    loads[0].wait()
    own_heads = rows_of(heads, 0, heads.shape[2]).astype(jnp.bfloat16)
    attn_rows = reduce_scatter(
        0,
        lambda k: jnp.dot(
            own_heads, w_proj[:, k * part : (k + 1) * part], preferred_element_type=jnp.float32
        ),
    )

    mid_state = (hidden_in[...].astype(jnp.float32) + attn_rows).astype(jnp.bfloat16)
    mid_wide = mid_state.astype(jnp.float32)
    scale = lax.rsqrt(jnp.mean(mid_wide * mid_wide, axis=-1, keepdims=True) + 1e-06)
    gathered[my_slot, :, :width] = (mid_wide * scale * norm_gain[...]).astype(jnp.bfloat16)

    @pl.loop(1, chips)
    def _(step):
        to = lax.rem(chip + step, chips)
        pltpu.make_async_remote_copy(
            src_ref=gathered.at[my_slot],
            dst_ref=gathered.at[my_slot],
            send_sem=ag_send,
            recv_sem=ag_recv.at[chip],
            device_id={"tensor": to * 2 + core},
            device_id_type=MESH,
        ).start()

    def relay(index):
        pltpu.make_async_remote_copy(
            src_ref=gathered.at[index],
            dst_ref=gathered.at[index],
            send_sem=relay_send,
            recv_sem=relay_recv,
            device_id={"tensor": partner},
            device_id_type=MESH,
        ).start()

    relay(my_slot)

    @pl.loop(1, chips)
    def _(step):
        source = lax.rem(chip + step, chips)
        index = core * chips + source
        wait_bytes(gathered.at[index], ag_recv.at[source])
        relay(index)

    wait_bytes(gathered.at[pl.ds(0, chips)], relay_recv)

    lane = lax.broadcasted_iota(jnp.int32, (2 * half, pad), 1)
    share = jnp.sum(
        jnp.where(lane == me, rows_of(gathered, width, width + pad), 0.0), axis=-1, keepdims=True
    )
    rows_in = rows_of(gathered, 0, width).astype(jnp.bfloat16)
    loads[1].wait()
    piece = 256
    for lo in range(0, ff, piece):
        gate_part = jnp.dot(
            rows_in, w_in[:, lo : lo + piece], preferred_element_type=jnp.float32
        )
        up_part = jnp.dot(
            rows_in, w_in[:, ff + lo : ff + lo + piece], preferred_element_type=jnp.float32
        )
        act[:, lo : lo + piece] = (gate_part / (1.0 + jnp.exp(-gate_part)) * up_part).astype(
            jnp.bfloat16
        )
    loads[2].wait()

    def expert_term(k):
        result = jnp.dot(
            act[...], w_out[:, k * part : (k + 1) * part], preferred_element_type=jnp.float32
        )
        return result.astype(jnp.bfloat16).astype(jnp.float32) * share

    moe_total = reduce_scatter(1, expert_term)
    hidden_out[...] = (mid_wide + moe_total).astype(jnp.bfloat16)

    wait_bytes(heads.at[pl.ds(0, n - 1)], head_send)
    for r in range(2):
        for k in range(CHUNKS):
            core_copy(r, k).wait_send()
        wait_bytes(chip_out.at[r, :, pl.ds(0, chips - 1)], chip_send.at[r])
    wait_bytes(gathered.at[pl.ds(0, chips - 1)], ag_send)
    wait_bytes(gathered.at[pl.ds(0, chips)], relay_send)


def layer(n, by_head, hidden_in, norm_gain, route_logits, expert_ids, weights):
    tokens, width = hidden_in.shape
    out_weight, expert_in, expert_out = weights
    ff = expert_out.shape[1]
    chips = n // 2
    pad = -(-n // 128) * 128
    part = width // CHUNKS
    bf16, f32 = jnp.bfloat16, jnp.float32
    vmem = pl.BlockSpec(memory_space=pltpu.VMEM)
    hbm = pl.BlockSpec(memory_space=pl.ANY)
    dma = pltpu.SemaphoreType.DMA
    return pl.pallas_call(
        functools.partial(layer_kernel, n),
        out_shape=jax.ShapeDtypeStruct((tokens, width), bf16),
        in_specs=[vmem] * 5 + [hbm] * 3,
        out_specs=vmem,
        scratch_shapes=[
            pltpu.VMEM(out_weight.shape, bf16),
            pltpu.VMEM(expert_in.shape[1:], bf16),
            pltpu.VMEM(expert_out.shape[1:], bf16),
            pltpu.VMEM(by_head.shape, bf16),
            pltpu.VMEM((2, CHUNKS, chips, tokens, part), bf16),
            pltpu.VMEM((2, CHUNKS, chips, tokens, part), bf16),
            pltpu.VMEM((CHUNKS, chips, tokens, part), f32),
            pltpu.VMEM((2, CHUNKS, chips, tokens, part), bf16),
            pltpu.VMEM((2, CHUNKS, chips, tokens, part), bf16),
            pltpu.VMEM((n, tokens, width + pad), bf16),
            pltpu.VMEM((n * tokens, ff), bf16),
            dma((3,)),
            dma,
            dma,
            dma((2, CHUNKS)),
            dma((2, CHUNKS)),
            dma((2,)),
            dma((2, CHUNKS)),
            dma,
            dma((chips,)),
            dma,
            dma,
        ],
        compiler_params=pltpu.CompilerParams(
            collective_id=0, has_side_effects=True, vmem_limit_bytes=60 * 1024 * 1024
        ),
        name="layer",
    )(by_head, hidden_in, norm_gain, route_logits, expert_ids, out_weight, expert_in, expert_out)


def on_device(
    hidden_in,
    queries,
    kv_cache,
    new_kv,
    cycle_pos,
    out_weight,
    norm_gain,
    route_logits,
    expert_ids,
    expert_in,
    expert_out,
):
    devices = lax.axis_size("tensor")
    device_index = lax.axis_index("tensor")
    rows_here, slots, _ = kv_cache.shape
    local_tokens = hidden_in.shape[0]
    kv_heads = rows_here // local_tokens
    per_kv = queries.shape[1] // HD
    head_dev = kv_heads * per_kv // devices
    own_pos = lax.dynamic_slice_in_dim(cycle_pos, device_index * local_tokens, local_tokens)
    positions = jnp.repeat(own_pos, kv_heads) + SINK
    write_mask = lax.broadcasted_iota(jnp.int32, (rows_here, slots), 1) == positions[:, None]
    new_cache = jnp.where(write_mask[:, :, None], new_kv[:, None, :], kv_cache)
    key_part = new_cache[:, :, :HD]
    value_part = new_cache[:, :, HD:]
    query_heads = queries.reshape(rows_here, per_kv, HD)
    scores = jnp.einsum(
        "rqk,rsk->rqs", query_heads, key_part, preferred_element_type=jnp.float32
    ) / math.sqrt(HD)
    peak = jnp.max(scores, axis=-1, keepdims=True)
    weights = jnp.exp(scores - peak)
    attn_probs = (weights / jnp.sum(weights, axis=-1, keepdims=True)).astype(jnp.bfloat16)
    head_out = jnp.einsum(
        "rqs,rsk->rqk", attn_probs, value_part, preferred_element_type=jnp.float32
    ).astype(jnp.bfloat16)
    by_head = head_out.reshape(local_tokens, devices, head_dev * HD).transpose(1, 0, 2)
    hidden_out = layer(
        devices,
        by_head,
        hidden_in,
        norm_gain.reshape(1, -1),
        route_logits,
        expert_ids,
        (out_weight, expert_in, expert_out),
    )
    return (hidden_out, new_cache)


def solution(mesh):
    return jax.shard_map(
        on_device,
        mesh=mesh,
        in_specs=(
            P(("group", "tensor"), None),
            P(("group", "tensor"), None),
            P(("group", "tensor"), None, None),
            P(("group", "tensor"), None),
            P("group"),
            P("tensor", None),
            P(),
            P(("group", "tensor"), None),
            P(("group", "tensor"), None),
            P("tensor", None, None),
            P("tensor", None, None),
        ),
        out_specs=(P(("group", "tensor"), None), P(("group", "tensor"), None, None)),
        check_vma=False,
    )
```

```python
import functools
import math

import jax
import jax.numpy as jnp
from jax import lax
from jax.experimental import pallas as pl
from jax.experimental.pallas import tpu as pltpu
from jax.sharding import PartitionSpec as P

HD = 128
SINK = 4
MESH = pl.DeviceIdType.MESH


def wait_bytes(ref, sem):
    pltpu.make_async_copy(ref, ref, sem).wait()


def layer_kernel(
    n,
    queries,
    hidden_in,
    norm_gain,
    route_logits,
    expert_ids,
    new_cache,
    out_weight,
    expert_in,
    expert_out,
    hidden_out,
    w_proj,
    w_in,
    w_out,
    cache,
    query_rows,
    score_rows,
    out_rows,
    by_head,
    heads,
    core_out,
    core_in,
    mine,
    chip_out,
    chip_in,
    gathered,
    act,
    load_sem,
    head_send,
    head_recv,
    core_send,
    core_recv,
    chip_send,
    chip_recv,
    ag_send,
    ag_recv,
    relay_send,
    relay_recv,
):
    me = lax.axis_index("tensor")
    chips = n // 2
    chip, core = me // 2, me % 2
    partner = chip * 2 + (1 - core)
    tokens, width = hidden_in.shape
    ff = w_out.shape[0]
    half = chips * tokens

    barrier = pltpu.get_barrier_semaphore()

    @pl.loop(1, n)
    def _(k):
        pl.semaphore_signal(
            barrier, inc=1, device_id={"tensor": lax.rem(me + k, n)}, device_id_type=MESH
        )

    cache_load = pltpu.make_async_copy(new_cache, cache, load_sem.at[3])
    cache_load.start()
    loads = [
        pltpu.make_async_copy(out_weight, w_proj, load_sem.at[0]),
        pltpu.make_async_copy(expert_in.at[0], w_in, load_sem.at[1]),
        pltpu.make_async_copy(expert_out.at[0], w_out, load_sem.at[2]),
    ]
    for load in loads:
        load.start()

    rows_here = cache.shape[0]
    kv_heads = rows_here // tokens
    per_kv = queries.shape[1] // HD
    for h in range(per_kv):
        query_rows[h * rows_here : (h + 1) * rows_here, :] = queries[
            :, h * HD : (h + 1) * HD
        ].astype(jnp.float32)
    cache_load.wait()
    for r in range(rows_here):
        query = query_rows[pl.ds(r, per_kv, stride=rows_here), :].astype(jnp.bfloat16)
        score_rows[r * per_kv : (r + 1) * per_kv, :] = lax.dot_general(
            query,
            cache[r, :, :HD],
            (((1,), (1,)), ((), ())),
            preferred_element_type=jnp.float32,
        )
    scores = score_rows[...] / math.sqrt(HD)
    powers = jnp.exp(scores - jnp.max(scores, axis=-1, keepdims=True))
    score_rows[...] = powers / jnp.sum(powers, axis=-1, keepdims=True)
    for r in range(rows_here):
        probs = score_rows[r * per_kv : (r + 1) * per_kv, :].astype(jnp.bfloat16)
        first = (r % kv_heads) * per_kv * tokens + r // kv_heads
        out_rows[pl.ds(first, per_kv, stride=tokens), :] = jnp.dot(
            probs, cache[r, :, HD:], preferred_element_type=jnp.float32
        )
    by_head[...] = out_rows[...].reshape(by_head.shape).astype(jnp.bfloat16)

    pl.semaphore_wait(barrier, n - 1)

    def slot(device):
        return lax.rem(device, 2) * chips + device // 2

    my_slot = slot(me)

    @pl.loop(1, n)
    def _(k):
        to = lax.rem(me + k, n)
        pltpu.make_async_remote_copy(
            src_ref=by_head.at[to],
            dst_ref=heads.at[my_slot],
            send_sem=head_send,
            recv_sem=head_recv,
            device_id={"tensor": to},
            device_id_type=MESH,
        ).start()

    heads[my_slot] = by_head[me]

    logits = route_logits[...]
    top = logits.shape[1]
    powers = jnp.exp(logits - jnp.max(logits, axis=-1, keepdims=True))
    gate = (powers / jnp.sum(powers, axis=-1, keepdims=True)).astype(jnp.bfloat16)
    gate = gate.astype(jnp.float32)
    pad = gathered.shape[2] - width
    lanes = lax.broadcasted_iota(jnp.int32, (tokens, pad), 1)
    ids = expert_ids[...]
    table = jnp.zeros((tokens, pad), jnp.float32)
    for j in range(top):
        table = table + jnp.where(lanes == ids[:, j : j + 1], gate[:, j : j + 1], 0.0)
    gathered[my_slot, :, width:] = table.astype(jnp.bfloat16)

    def rows_of(ref, lo, hi):
        other = ref[pl.ds((1 - core) * chips, chips), :, lo:hi].astype(jnp.float32)
        own = ref[pl.ds(core * chips, chips), :, lo:hi].astype(jnp.float32)
        return jnp.concatenate(
            [other.reshape(half, hi - lo), own.reshape(half, hi - lo)], axis=0
        )

    def head_rows(parity):
        block = heads[pl.ds(parity * chips, chips)].astype(jnp.float32)
        return jnp.concatenate(
            [block[:, h].reshape(half, HD) for h in range(heads.shape[1])], axis=-1
        ).astype(jnp.bfloat16)

    def core_copy(r):
        return pltpu.make_async_remote_copy(
            src_ref=core_out.at[r],
            dst_ref=core_in.at[r],
            send_sem=core_send.at[r],
            recv_sem=core_recv.at[r],
            device_id={"tensor": partner},
            device_id_type=MESH,
        )

    def reduce_scatter(r, other_term, own_term):
        core_out[r] = other_term().reshape(chips, tokens, width).astype(jnp.bfloat16)
        core_copy(r).start()
        mine[...] = own_term().reshape(chips, tokens, width)
        core_copy(r).wait_recv()

        def total(to):
            return (mine[to] + core_in[r, to].astype(jnp.float32)).astype(jnp.bfloat16)

        @pl.loop(1, chips)
        def _(step):
            to = lax.rem(chip + step, chips)
            chip_out[r, to] = total(to)
            pltpu.make_async_remote_copy(
                src_ref=chip_out.at[r, to],
                dst_ref=chip_in.at[r, chip],
                send_sem=chip_send.at[r],
                recv_sem=chip_recv.at[r],
                device_id={"tensor": to * 2 + core},
                device_id_type=MESH,
            ).start()

        chip_in[r, chip] = total(chip)
        wait_bytes(chip_in.at[r, pl.ds(0, chips - 1)], chip_recv.at[r])
        return jnp.sum(chip_in[r].astype(jnp.float32), axis=0)

    wait_bytes(heads.at[pl.ds(0, n - 1)], head_recv)
    loads[0].wait()

    def projected(parity):
        return jnp.dot(head_rows(parity), w_proj[...], preferred_element_type=jnp.float32)

    attn_rows = reduce_scatter(0, lambda: projected(1 - core), lambda: projected(core))

    mid_state = (hidden_in[...].astype(jnp.float32) + attn_rows).astype(jnp.bfloat16)
    mid_wide = mid_state.astype(jnp.float32)
    scale = lax.rsqrt(jnp.mean(mid_wide * mid_wide, axis=-1, keepdims=True) + 1e-06)
    gathered[my_slot, :, :width] = (mid_wide * scale * norm_gain[...]).astype(jnp.bfloat16)

    @pl.loop(1, chips)
    def _(step):
        to = lax.rem(chip + step, chips)
        pltpu.make_async_remote_copy(
            src_ref=gathered.at[my_slot],
            dst_ref=gathered.at[my_slot],
            send_sem=ag_send,
            recv_sem=ag_recv.at[chip],
            device_id={"tensor": to * 2 + core},
            device_id_type=MESH,
        ).start()

    def relay(index):
        pltpu.make_async_remote_copy(
            src_ref=gathered.at[index],
            dst_ref=gathered.at[index],
            send_sem=relay_send,
            recv_sem=relay_recv,
            device_id={"tensor": partner},
            device_id_type=MESH,
        ).start()

    relay(my_slot)

    @pl.loop(1, chips)
    def _(step):
        source = lax.rem(chip + step, chips)
        index = core * chips + source
        wait_bytes(gathered.at[index], ag_recv.at[source])
        relay(index)

    wait_bytes(gathered.at[pl.ds(0, chips)], relay_recv)

    lane = lax.broadcasted_iota(jnp.int32, (2 * half, pad), 1)
    share = jnp.sum(
        jnp.where(lane == me, rows_of(gathered, width, width + pad), 0.0), axis=-1, keepdims=True
    )
    rows_in = rows_of(gathered, 0, width).astype(jnp.bfloat16)
    loads[1].wait()
    piece = 256
    for lo in range(0, ff, piece):
        gate_part = jnp.dot(
            rows_in, w_in[:, lo : lo + piece], preferred_element_type=jnp.float32
        )
        up_part = jnp.dot(
            rows_in, w_in[:, ff + lo : ff + lo + piece], preferred_element_type=jnp.float32
        )
        act[:, lo : lo + piece] = (gate_part / (1.0 + jnp.exp(-gate_part)) * up_part).astype(
            jnp.bfloat16
        )
    loads[2].wait()

    def expert_term(lo):
        result = jnp.dot(
            act[lo : lo + half, :], w_out[...], preferred_element_type=jnp.float32
        )
        return result.astype(jnp.bfloat16).astype(jnp.float32) * share[lo : lo + half]

    moe_total = reduce_scatter(1, lambda: expert_term(0), lambda: expert_term(half))
    hidden_out[...] = (mid_wide + moe_total).astype(jnp.bfloat16)

    wait_bytes(heads.at[pl.ds(0, n - 1)], head_send)
    for r in range(2):
        core_copy(r).wait_send()
        wait_bytes(chip_out.at[r, pl.ds(0, chips - 1)], chip_send.at[r])
    wait_bytes(gathered.at[pl.ds(0, chips - 1)], ag_send)
    wait_bytes(gathered.at[pl.ds(0, chips)], relay_send)


def layer(n, queries, hidden_in, norm_gain, route_logits, expert_ids, new_cache, weights):
    tokens, width = hidden_in.shape
    out_weight, expert_in, expert_out = weights
    ff = expert_out.shape[1]
    chips = n // 2
    pad = -(-n // 128) * 128
    rows_here, slots, _ = new_cache.shape
    heads_all = rows_here // tokens * (queries.shape[1] // HD)
    exchange = (n, heads_all // n, tokens, HD)
    bf16, f32 = jnp.bfloat16, jnp.float32
    vmem = pl.BlockSpec(memory_space=pltpu.VMEM)
    hbm = pl.BlockSpec(memory_space=pl.ANY)
    dma = pltpu.SemaphoreType.DMA
    return pl.pallas_call(
        functools.partial(layer_kernel, n),
        out_shape=jax.ShapeDtypeStruct((tokens, width), bf16),
        in_specs=[vmem] * 5 + [hbm] * 4,
        out_specs=vmem,
        scratch_shapes=[
            pltpu.VMEM(out_weight.shape, bf16),
            pltpu.VMEM(expert_in.shape[1:], bf16),
            pltpu.VMEM(expert_out.shape[1:], bf16),
            pltpu.VMEM(new_cache.shape, bf16),
            pltpu.VMEM((heads_all * tokens, HD), f32),
            pltpu.VMEM((heads_all * tokens, slots), f32),
            pltpu.VMEM((heads_all * tokens, HD), f32),
            pltpu.VMEM(exchange, bf16),
            pltpu.VMEM(exchange, bf16),
            pltpu.VMEM((2, chips, tokens, width), bf16),
            pltpu.VMEM((2, chips, tokens, width), bf16),
            pltpu.VMEM((chips, tokens, width), f32),
            pltpu.VMEM((2, chips, tokens, width), bf16),
            pltpu.VMEM((2, chips, tokens, width), bf16),
            pltpu.VMEM((n, tokens, width + pad), bf16),
            pltpu.VMEM((n * tokens, ff), bf16),
            dma((4,)),
            dma,
            dma,
            dma((2,)),
            dma((2,)),
            dma((2,)),
            dma((2,)),
            dma,
            dma((chips,)),
            dma,
            dma,
        ],
        compiler_params=pltpu.CompilerParams(
            collective_id=0, has_side_effects=True, vmem_limit_bytes=60 * 1024 * 1024
        ),
        name="layer",
    )(
        queries,
        hidden_in,
        norm_gain,
        route_logits,
        expert_ids,
        new_cache,
        out_weight,
        expert_in,
        expert_out,
    )


def on_device(
    hidden_in,
    queries,
    kv_cache,
    new_kv,
    cycle_pos,
    out_weight,
    norm_gain,
    route_logits,
    expert_ids,
    expert_in,
    expert_out,
):
    devices = lax.axis_size("tensor")
    device_index = lax.axis_index("tensor")
    rows_here, slots, _ = kv_cache.shape
    local_tokens = hidden_in.shape[0]
    kv_heads = rows_here // local_tokens
    own_pos = lax.dynamic_slice_in_dim(cycle_pos, device_index * local_tokens, local_tokens)
    grouped = (local_tokens, kv_heads, slots, 2 * HD)
    written = lax.broadcasted_iota(jnp.int32, grouped, 2) == (own_pos + SINK)[:, None, None, None]
    new_cache = jnp.where(
        written,
        new_kv.reshape(local_tokens, kv_heads, 1, 2 * HD),
        kv_cache.reshape(grouped),
    ).reshape(kv_cache.shape)
    hidden_out = layer(
        devices,
        queries,
        hidden_in,
        norm_gain.reshape(1, -1),
        route_logits,
        expert_ids,
        new_cache,
        (out_weight, expert_in, expert_out),
    )
    return (hidden_out, new_cache)


def solution(mesh):
    return jax.shard_map(
        on_device,
        mesh=mesh,
        in_specs=(
            P(("group", "tensor"), None),
            P(("group", "tensor"), None),
            P(("group", "tensor"), None, None),
            P(("group", "tensor"), None),
            P("group"),
            P("tensor", None),
            P(),
            P(("group", "tensor"), None),
            P(("group", "tensor"), None),
            P("tensor", None, None),
            P("tensor", None, None),
        ),
        out_specs=(P(("group", "tensor"), None), P(("group", "tensor"), None, None)),
        check_vma=False,
    )
```

```python
import functools
import math

import jax
import jax.numpy as jnp
from jax import lax
from jax.experimental import pallas as pl
from jax.experimental.pallas import tpu as pltpu
from jax.sharding import PartitionSpec as P

HD = 128
SINK = 4
MESH = pl.DeviceIdType.MESH


def wait_bytes(ref, sem):
    pltpu.make_async_copy(ref, ref, sem).wait()


def layer_kernel(
    n,
    queries,
    hidden_in,
    norm_gain,
    route_logits,
    expert_ids,
    new_kv,
    cycle_pos,
    kv_cache,
    out_weight,
    expert_in,
    expert_out,
    hidden_out,
    new_cache,
    w_proj,
    w_in,
    w_out,
    cache,
    query_rows,
    score_rows,
    out_rows,
    by_head,
    heads,
    core_out,
    core_in,
    mine,
    chip_out,
    chip_in,
    gathered,
    act,
    load_sem,
    head_send,
    head_recv,
    core_send,
    core_recv,
    chip_send,
    chip_recv,
    ag_send,
    ag_recv,
    relay_send,
    relay_recv,
):
    me = lax.axis_index("tensor")
    chips = n // 2
    chip, core = me // 2, me % 2
    partner = chip * 2 + (1 - core)
    tokens, width = hidden_in.shape
    ff = w_out.shape[0]
    half = chips * tokens

    barrier = pltpu.get_barrier_semaphore()

    @pl.loop(1, n)
    def _(k):
        pl.semaphore_signal(
            barrier, inc=1, device_id={"tensor": lax.rem(me + k, n)}, device_id_type=MESH
        )

    cache_load = pltpu.make_async_copy(kv_cache, cache, load_sem.at[3])
    cache_load.start()
    loads = [
        pltpu.make_async_copy(out_weight, w_proj, load_sem.at[0]),
        pltpu.make_async_copy(expert_in.at[0], w_in, load_sem.at[1]),
        pltpu.make_async_copy(expert_out.at[0], w_out, load_sem.at[2]),
    ]
    for load in loads:
        load.start()

    rows_here = cache.shape[0]
    kv_heads = rows_here // tokens
    per_kv = queries.shape[1] // HD
    for h in range(per_kv):
        query_rows[h * rows_here : (h + 1) * rows_here, :] = queries[
            :, h * HD : (h + 1) * HD
        ].astype(jnp.float32)
    cache_load.wait()
    slot_ids = lax.broadcasted_iota(jnp.int32, cache.shape[1:], 0)
    for t in range(tokens):
        written = slot_ids == cycle_pos[me * tokens + t] + SINK
        for r in range(t * kv_heads, (t + 1) * kv_heads):
            cache[r] = jnp.where(
                written, new_kv[r : r + 1, :].astype(jnp.float32), cache[r].astype(jnp.float32)
            ).astype(jnp.bfloat16)
    for r in range(rows_here):
        query = query_rows[pl.ds(r, per_kv, stride=rows_here), :].astype(jnp.bfloat16)
        score_rows[r * per_kv : (r + 1) * per_kv, :] = lax.dot_general(
            query,
            cache[r, :, :HD],
            (((1,), (1,)), ((), ())),
            preferred_element_type=jnp.float32,
        )
    scores = score_rows[...] / math.sqrt(HD)
    powers = jnp.exp(scores - jnp.max(scores, axis=-1, keepdims=True))
    score_rows[...] = powers / jnp.sum(powers, axis=-1, keepdims=True)
    cache_store = pltpu.make_async_copy(cache, new_cache, load_sem.at[4])
    cache_store.start()
    for r in range(rows_here):
        probs = score_rows[r * per_kv : (r + 1) * per_kv, :].astype(jnp.bfloat16)
        first = (r % kv_heads) * per_kv * tokens + r // kv_heads
        out_rows[pl.ds(first, per_kv, stride=tokens), :] = jnp.dot(
            probs, cache[r, :, HD:], preferred_element_type=jnp.float32
        )
    by_head[...] = out_rows[...].reshape(by_head.shape).astype(jnp.bfloat16)

    pl.semaphore_wait(barrier, n - 1)

    def slot(device):
        return lax.rem(device, 2) * chips + device // 2

    my_slot = slot(me)

    @pl.loop(1, n)
    def _(k):
        to = lax.rem(me + k, n)
        pltpu.make_async_remote_copy(
            src_ref=by_head.at[to],
            dst_ref=heads.at[my_slot],
            send_sem=head_send,
            recv_sem=head_recv,
            device_id={"tensor": to},
            device_id_type=MESH,
        ).start()

    heads[my_slot] = by_head[me]

    logits = route_logits[...]
    top = logits.shape[1]
    powers = jnp.exp(logits - jnp.max(logits, axis=-1, keepdims=True))
    gate = (powers / jnp.sum(powers, axis=-1, keepdims=True)).astype(jnp.bfloat16)
    gate = gate.astype(jnp.float32)
    pad = gathered.shape[2] - width
    lanes = lax.broadcasted_iota(jnp.int32, (tokens, pad), 1)
    ids = expert_ids[...]
    table = jnp.zeros((tokens, pad), jnp.float32)
    for j in range(top):
        table = table + jnp.where(lanes == ids[:, j : j + 1], gate[:, j : j + 1], 0.0)
    gathered[my_slot, :, width:] = table.astype(jnp.bfloat16)

    def rows_of(ref, lo, hi):
        other = ref[pl.ds((1 - core) * chips, chips), :, lo:hi].astype(jnp.float32)
        own = ref[pl.ds(core * chips, chips), :, lo:hi].astype(jnp.float32)
        return jnp.concatenate(
            [other.reshape(half, hi - lo), own.reshape(half, hi - lo)], axis=0
        )

    def head_rows(parity):
        block = heads[pl.ds(parity * chips, chips)].astype(jnp.float32)
        return jnp.concatenate(
            [block[:, h].reshape(half, HD) for h in range(heads.shape[1])], axis=-1
        ).astype(jnp.bfloat16)

    def core_copy(r):
        return pltpu.make_async_remote_copy(
            src_ref=core_out.at[r],
            dst_ref=core_in.at[r],
            send_sem=core_send.at[r],
            recv_sem=core_recv.at[r],
            device_id={"tensor": partner},
            device_id_type=MESH,
        )

    def reduce_scatter(r, other_term, own_term):
        core_out[r] = other_term().reshape(chips, tokens, width).astype(jnp.bfloat16)
        core_copy(r).start()
        mine[...] = own_term().reshape(chips, tokens, width)
        core_copy(r).wait_recv()

        def total(to):
            return (mine[to] + core_in[r, to].astype(jnp.float32)).astype(jnp.bfloat16)

        @pl.loop(1, chips)
        def _(step):
            to = lax.rem(chip + step, chips)
            chip_out[r, to] = total(to)
            pltpu.make_async_remote_copy(
                src_ref=chip_out.at[r, to],
                dst_ref=chip_in.at[r, chip],
                send_sem=chip_send.at[r],
                recv_sem=chip_recv.at[r],
                device_id={"tensor": to * 2 + core},
                device_id_type=MESH,
            ).start()

        chip_in[r, chip] = total(chip)
        wait_bytes(chip_in.at[r, pl.ds(0, chips - 1)], chip_recv.at[r])
        return jnp.sum(chip_in[r].astype(jnp.float32), axis=0)

    wait_bytes(heads.at[pl.ds(0, n - 1)], head_recv)
    loads[0].wait()

    def projected(parity):
        return jnp.dot(head_rows(parity), w_proj[...], preferred_element_type=jnp.float32)

    attn_rows = reduce_scatter(0, lambda: projected(1 - core), lambda: projected(core))

    mid_state = (hidden_in[...].astype(jnp.float32) + attn_rows).astype(jnp.bfloat16)
    mid_wide = mid_state.astype(jnp.float32)
    scale = lax.rsqrt(jnp.mean(mid_wide * mid_wide, axis=-1, keepdims=True) + 1e-06)
    gathered[my_slot, :, :width] = (mid_wide * scale * norm_gain[...]).astype(jnp.bfloat16)

    @pl.loop(1, chips)
    def _(step):
        to = lax.rem(chip + step, chips)
        pltpu.make_async_remote_copy(
            src_ref=gathered.at[my_slot],
            dst_ref=gathered.at[my_slot],
            send_sem=ag_send,
            recv_sem=ag_recv.at[chip],
            device_id={"tensor": to * 2 + core},
            device_id_type=MESH,
        ).start()

    def relay(index):
        pltpu.make_async_remote_copy(
            src_ref=gathered.at[index],
            dst_ref=gathered.at[index],
            send_sem=relay_send,
            recv_sem=relay_recv,
            device_id={"tensor": partner},
            device_id_type=MESH,
        ).start()

    relay(my_slot)

    @pl.loop(1, chips)
    def _(step):
        source = lax.rem(chip + step, chips)
        index = core * chips + source
        wait_bytes(gathered.at[index], ag_recv.at[source])
        relay(index)

    wait_bytes(gathered.at[pl.ds(0, chips)], relay_recv)

    lane = lax.broadcasted_iota(jnp.int32, (2 * half, pad), 1)
    share = jnp.sum(
        jnp.where(lane == me, rows_of(gathered, width, width + pad), 0.0), axis=-1, keepdims=True
    )
    rows_in = rows_of(gathered, 0, width).astype(jnp.bfloat16)
    loads[1].wait()
    piece = 256
    for lo in range(0, ff, piece):
        gate_part = jnp.dot(
            rows_in, w_in[:, lo : lo + piece], preferred_element_type=jnp.float32
        )
        up_part = jnp.dot(
            rows_in, w_in[:, ff + lo : ff + lo + piece], preferred_element_type=jnp.float32
        )
        act[:, lo : lo + piece] = (gate_part / (1.0 + jnp.exp(-gate_part)) * up_part).astype(
            jnp.bfloat16
        )
    loads[2].wait()

    def expert_term(lo):
        result = jnp.dot(
            act[lo : lo + half, :], w_out[...], preferred_element_type=jnp.float32
        )
        return result.astype(jnp.bfloat16).astype(jnp.float32) * share[lo : lo + half]

    moe_total = reduce_scatter(1, lambda: expert_term(0), lambda: expert_term(half))
    hidden_out[...] = (mid_wide + moe_total).astype(jnp.bfloat16)

    cache_store.wait()
    wait_bytes(heads.at[pl.ds(0, n - 1)], head_send)
    for r in range(2):
        core_copy(r).wait_send()
        wait_bytes(chip_out.at[r, pl.ds(0, chips - 1)], chip_send.at[r])
    wait_bytes(gathered.at[pl.ds(0, chips - 1)], ag_send)
    wait_bytes(gathered.at[pl.ds(0, chips)], relay_send)


def layer(n, queries, hidden_in, norm_gain, route_logits, expert_ids, new_kv, cycle_pos, kv_cache, weights):
    tokens, width = hidden_in.shape
    out_weight, expert_in, expert_out = weights
    ff = expert_out.shape[1]
    chips = n // 2
    pad = -(-n // 128) * 128
    rows_here, slots, _ = kv_cache.shape
    heads_all = rows_here // tokens * (queries.shape[1] // HD)
    exchange = (n, heads_all // n, tokens, HD)
    bf16, f32 = jnp.bfloat16, jnp.float32
    vmem = pl.BlockSpec(memory_space=pltpu.VMEM)
    hbm = pl.BlockSpec(memory_space=pl.ANY)
    dma = pltpu.SemaphoreType.DMA
    return pl.pallas_call(
        functools.partial(layer_kernel, n),
        out_shape=(
            jax.ShapeDtypeStruct((tokens, width), bf16),
            jax.ShapeDtypeStruct(kv_cache.shape, bf16),
        ),
        in_specs=[vmem] * 6 + [pl.BlockSpec(memory_space=pltpu.SMEM)] + [hbm] * 4,
        out_specs=(vmem, hbm),
        scratch_shapes=[
            pltpu.VMEM(out_weight.shape, bf16),
            pltpu.VMEM(expert_in.shape[1:], bf16),
            pltpu.VMEM(expert_out.shape[1:], bf16),
            pltpu.VMEM(kv_cache.shape, bf16),
            pltpu.VMEM((heads_all * tokens, HD), f32),
            pltpu.VMEM((heads_all * tokens, slots), f32),
            pltpu.VMEM((heads_all * tokens, HD), f32),
            pltpu.VMEM(exchange, bf16),
            pltpu.VMEM(exchange, bf16),
            pltpu.VMEM((2, chips, tokens, width), bf16),
            pltpu.VMEM((2, chips, tokens, width), bf16),
            pltpu.VMEM((chips, tokens, width), f32),
            pltpu.VMEM((2, chips, tokens, width), bf16),
            pltpu.VMEM((2, chips, tokens, width), bf16),
            pltpu.VMEM((n, tokens, width + pad), bf16),
            pltpu.VMEM((n * tokens, ff), bf16),
            dma((5,)),
            dma,
            dma,
            dma((2,)),
            dma((2,)),
            dma((2,)),
            dma((2,)),
            dma,
            dma((chips,)),
            dma,
            dma,
        ],
        compiler_params=pltpu.CompilerParams(
            collective_id=0, has_side_effects=True, vmem_limit_bytes=60 * 1024 * 1024
        ),
        name="layer",
    )(
        queries,
        hidden_in,
        norm_gain,
        route_logits,
        expert_ids,
        new_kv,
        cycle_pos,
        kv_cache,
        out_weight,
        expert_in,
        expert_out,
    )


def on_device(
    hidden_in,
    queries,
    kv_cache,
    new_kv,
    cycle_pos,
    out_weight,
    norm_gain,
    route_logits,
    expert_ids,
    expert_in,
    expert_out,
):
    devices = lax.axis_size("tensor")
    return layer(
        devices,
        queries,
        hidden_in,
        norm_gain.reshape(1, -1),
        route_logits,
        expert_ids,
        new_kv,
        cycle_pos,
        kv_cache,
        (out_weight, expert_in, expert_out),
    )


def solution(mesh):
    return jax.shard_map(
        on_device,
        mesh=mesh,
        in_specs=(
            P(("group", "tensor"), None),
            P(("group", "tensor"), None),
            P(("group", "tensor"), None, None),
            P(("group", "tensor"), None),
            P("group"),
            P("tensor", None),
            P(),
            P(("group", "tensor"), None),
            P(("group", "tensor"), None),
            P("tensor", None, None),
            P("tensor", None, None),
        ),
        out_specs=(P(("group", "tensor"), None), P(("group", "tensor"), None, None)),
        check_vma=False,
    )
```
